512 devices in a mesh: dom: 16 (over x_lo, y), gx: 4 (over x_hi, core), gy: 8 (over z).
Axes of the slice: x: 4 (x_hi: 2, x_lo: 2; x = x_hi * 2 + x_lo), y: 8, z: 8, core: 2. Of those that a mesh axis runs over, the one named last changes fastest.
Arguments:
- ensemble: float32 [16, 4, 32, 32, 1024], P('dom', None, None, 'gx', 'gy'), may hold values from -6 to 6
- ancestors: int32 [16, 4, 128], P(None, 'gx', 'gy'), may hold values from 0 to 15
- particle_air_drag: float32 [16, 2, 32, 1024], P('dom', None, 'gx', 'gy'), may hold values from -6 to 6
- eddy_diffusivity: float32 [31], replicated, may hold values from 0.02 to 0.15
Outputs:
- forecast: float32 [16, 4, 32, 32, 1024], P('dom', None, None, 'gx', 'gy')
The draws below stay inside these ranges and needn't reach their ends.
All inputs are finite; a program needn't handle non-finite values.
Results may differ from the reference program's by a relative error of at most 0.0003.
Values sent between devices are 32-bit elements; how exact they have to be, the bound alone decides.
No kernel may reach another device: no remote copies, remote signals or barrier semaphores. Data moves between devices by JAX's collectives and lax.ppermute only.
A program may use at most 64 MiB of HBM per device.

```python
import math
import jax
import jax.numpy as jnp
import numpy as np
from jax import lax

FIELDS = 4
LEV = 32
STEPS = 4
TILE = 8
PARTICLES = 16
NX = 32
NY = 1024
TILES_X = 4
TILES_Y = 128


def touch_ends(result, own_key, smallest, largest):
    spot = [jax.random.randint(jax.random.fold_in(own_key, axis), (), 0, length) for axis, length in enumerate(result.shape)]
    widest = result.shape.index(max(result.shape))
    neighbour = spot[:widest] + [(spot[widest] + 1) % result.shape[widest]] + spot[widest + 1:]
    return result.at[tuple(spot)].set(smallest).at[tuple(neighbour)].set(largest)


def level_of(key, extent, cuts, smallest, largest):
    level, own = 1.0, jax.random.fold_in(key, 6)
    for axis_at, blocks in cuts:
        draws = jnp.exp(jax.random.uniform(jax.random.fold_in(own, axis_at), (blocks,), jnp.float32, smallest / len(cuts), largest / len(cuts)))
        level = level * jnp.repeat(draws, extent[axis_at] // blocks).reshape([-1 if axis == axis_at else 1 for axis in range(len(extent))])
    return level


def cumulative_ranks(number_of, slope):
    weights = [(1 << 20) // math.isqrt(standing ** slope) + 1 for standing in range(1, number_of + 1)]
    width = 1 + sum(weights) // (1 << 30)
    return np.cumsum(np.array([max(1, weight // width) for weight in weights]))


def skewed_ids(own_key, extent, count, skew):
    listing = cumulative_ranks(count, skew)
    lot = jax.random.randint(jax.random.fold_in(own_key, 1), extent, 0, int(listing[count - 1]))
    standing = jnp.searchsorted(jnp.asarray(listing, jnp.int32), lot, side="right")
    return jax.random.permutation(jax.random.fold_in(own_key, 2), count)[standing].astype(jnp.int32)


def centred(own_key, extent, scale, most, split=(), held_as=jnp.bfloat16):
    factor_of = level_of(own_key, extent, split, -0.22, 0.18) if split else 1.0
    array = jax.random.normal(own_key, extent, jnp.float32) * scale * factor_of
    return jnp.minimum(jnp.maximum(array, -most), most).astype(held_as)


def setup_inputs(seed: int = 0) -> dict:
    seeds = jax.random.split(jax.random.key(seed), 5)
    return {
        "ensemble": centred(seeds[0], (PARTICLES, FIELDS, LEV, NX, NY), 1.0, 6.0, ((0, 16), (3, 4), (4, 8)), jnp.float32),
        "ancestors": touch_ends(skewed_ids(seeds[1], (PARTICLES, TILES_X, TILES_Y), PARTICLES, 2), jax.random.fold_in(seeds[1], 3), 0, PARTICLES - 1).astype(jnp.int32),
        "particle_air_drag": centred(seeds[2], (PARTICLES, 2, NX, NY), 1.0, 6.0, ((0, 16), (2, 4), (3, 8)), jnp.float32),
        "eddy_diffusivity": jnp.clip(jnp.exp(jax.random.uniform(seeds[3], (LEV - 1,), jnp.float32, math.log(0.02), math.log(0.15))), 0.02, 0.15),
    }


ADVECT = 0.2
DIFFUSE = 0.15
BUOY_TEMP = 0.2
BUOY_SALT = 0.1
PRESS_SCALE = 0.25
WIND_SCALE = 0.2
CORIO_BASE = 0.1
CORIO_SLOPE = 0.1


def advance(padded, topmost_slab, eddy_diffusivity, coriolis):
    centre = padded[:, :, 1:-1, 1:-1]
    eastern_neighbour_cell = padded[:, :, 2:, 1:-1]
    west_cell = padded[:, :, :-2, 1:-1]
    north_cell = padded[:, :, 1:-1, 2:]
    south_cell = padded[:, :, 1:-1, :-2]
    grad_x = 0.5 * (eastern_neighbour_cell - west_cell)
    grad_y = 0.5 * (north_cell - south_cell)
    spread = eastern_neighbour_cell + west_cell + north_cell + south_cell - 4.0 * centre
    buoyancy = BUOY_TEMP * padded[2] - BUOY_SALT * padded[3]
    pressure = PRESS_SCALE * jnp.cumsum(buoyancy, axis=0)
    press_x = 0.5 * (pressure[:, 2:, 1:-1] - pressure[:, :-2, 1:-1])
    press_y = 0.5 * (pressure[:, 1:-1, 2:] - pressure[:, 1:-1, :-2])
    vert_flux = eddy_diffusivity[None, :, None, None] * (centre[:, 1:] - centre[:, :-1])
    closed = jnp.zeros_like(centre[:, :1])
    vertical = jnp.concatenate([vert_flux, closed], axis=1) - jnp.concatenate([closed, vert_flux], axis=1)
    east_vel = centre[0]
    north_vel = centre[1]
    carried_over = east_vel[None] * grad_x + north_vel[None] * grad_y
    common = centre - ADVECT * carried_over + DIFFUSE * spread + vertical
    level_top = (jnp.arange(centre.shape[1]) == 0).astype(jnp.float32)[:, None, None]
    forcing = WIND_SCALE * topmost_slab[:, None] * level_top
    east_next = common[0] + coriolis * north_vel - press_x + forcing[0]
    north_next = common[1] - coriolis * east_vel - press_y + forcing[1]
    return jnp.stack([east_next, north_next, common[2], common[3]])


def march_prediction(marine_variables, topmost_slab, eddy_diffusivity):
    coriolis = CORIO_BASE + CORIO_SLOPE * (jnp.arange(NY, dtype=jnp.float32) + 0.5) / NY
    for iteration in range(STEPS):
        wrapped = jnp.concatenate([marine_variables[:, :, -1:], marine_variables, marine_variables[:, :, :1]], axis=2)
        padded = jnp.pad(wrapped, ((0, 0), (0, 0), (0, 0), (1, 1)))
        marine_variables = advance(padded, topmost_slab, eddy_diffusivity, coriolis)
    return marine_variables


def reference(ensemble, ancestors, particle_air_drag, eddy_diffusivity):
    cell_source = jnp.repeat(jnp.repeat(ancestors, TILE, axis=1), TILE, axis=2)

    def per_member(particle_number):
        source_map = cell_source[particle_number].astype(jnp.int32)
        gather_idx = jnp.broadcast_to(source_map[None, None, None], (1,) + ensemble.shape[1:])
        selected_particles = jnp.take_along_axis(ensemble, gather_idx, axis=0)[0]
        return march_prediction(selected_particles, particle_air_drag[particle_number], eddy_diffusivity)

    return lax.map(per_member, jnp.arange(PARTICLES, dtype=jnp.int32))
```

```python
import jax
import jax.numpy as jnp
from jax import lax
from jax.sharding import PartitionSpec as P

STEPS = 4
TILE = 8


ADVECT = 0.2
DIFFUSE = 0.15
BUOY_TEMP = 0.2
BUOY_SALT = 0.1
PRESS_SCALE = 0.25
WIND_SCALE = 0.2
CORIO_BASE = 0.1
CORIO_SLOPE = 0.1


def extended(x, sides, width, wrap):
    for axis, dim in sides:
        size, length = (lax.axis_size(axis), x.shape[dim])
        up = [(i, (i + 1) % size) for i in range(size if wrap else size - 1)]
        down = [(j, i) for i, j in up]
        last = lax.slice_in_dim(x, length - width, length, axis=dim)
        leading = lax.slice_in_dim(x, 0, width, axis=dim)
        before = lax.ppermute(last, axis, up)
        after = lax.ppermute(leading, axis, down)
        x = jnp.concatenate([before, x, after], axis=dim)
    return x


def advance(padded, topmost_slab, eddy_diffusivity, coriolis):
    centre = padded[:, :, 1:-1, 1:-1]
    eastern_neighbour_cell = padded[:, :, 2:, 1:-1]
    west_cell = padded[:, :, :-2, 1:-1]
    north_cell = padded[:, :, 1:-1, 2:]
    south_cell = padded[:, :, 1:-1, :-2]
    grad_x = 0.5 * (eastern_neighbour_cell - west_cell)
    grad_y = 0.5 * (north_cell - south_cell)
    spread = eastern_neighbour_cell + west_cell + north_cell + south_cell - 4.0 * centre
    buoyancy = BUOY_TEMP * padded[2] - BUOY_SALT * padded[3]
    pressure = PRESS_SCALE * jnp.cumsum(buoyancy, axis=0)
    press_x = 0.5 * (pressure[:, 2:, 1:-1] - pressure[:, :-2, 1:-1])
    press_y = 0.5 * (pressure[:, 1:-1, 2:] - pressure[:, 1:-1, :-2])
    vert_flux = eddy_diffusivity[None, :, None, None] * (centre[:, 1:] - centre[:, :-1])
    closed = jnp.zeros_like(centre[:, :1])
    vertical = jnp.concatenate([vert_flux, closed], axis=1) - jnp.concatenate(
        [closed, vert_flux], axis=1
    )
    east_vel = centre[0]
    north_vel = centre[1]
    carried_over = east_vel[None] * grad_x + north_vel[None] * grad_y
    common = centre - ADVECT * carried_over + DIFFUSE * spread + vertical
    level_top = (jnp.arange(centre.shape[1]) == 0).astype(jnp.float32)[:, None, None]
    forcing = WIND_SCALE * topmost_slab[:, None] * level_top
    east_next = common[0] + coriolis * north_vel - press_x + forcing[0]
    north_next = common[1] - coriolis * east_vel - press_y + forcing[1]
    return jnp.stack([east_next, north_next, common[2], common[3]])


def coriolis_at(positions, total_rows):
    return CORIO_BASE + CORIO_SLOPE * (positions.astype(jnp.float32) + 0.5) / total_rows


def resample(ensemble, ancestors):
    members = lax.axis_size("dom")
    block = ensemble[0]
    fields, levels, width_x, width_y = block.shape
    groups = fields * levels // members
    parts = block.reshape(members, groups, width_x, width_y)
    by_member = lax.all_to_all(parts, "dom", 0, 0, tiled=True)
    tiles = ancestors[:, 0, :]
    cell_source = jnp.repeat(tiles, TILE, 1)[:, None, None, :]
    picked = jnp.zeros_like(by_member)
    for member in range(members):
        picked = jnp.where(cell_source == member, by_member[member][None], picked)
    back = lax.all_to_all(picked, "dom", 0, 0, tiled=True)
    return back.reshape(fields, levels, width_x, width_y)


def per_device(ensemble, ancestors, particle_air_drag, eddy_diffusivity):
    width_y = ensemble.shape[4]
    selected_particles = resample(ensemble, ancestors)
    row_block = lax.axis_index("gy")
    total_rows = width_y * lax.axis_size("gy")
    topmost_slab = particle_air_drag[0]
    positions = row_block * width_y + jnp.arange(width_y, dtype=jnp.int32)
    coriolis = coriolis_at(positions, total_rows)
    marine_variables = selected_particles
    for iteration in range(STEPS):
        widened = extended(marine_variables, (("gx", 2),), 1, True)
        padded = extended(widened, (("gy", 3),), 1, False)
        marine_variables = advance(padded, topmost_slab, eddy_diffusivity, coriolis)
    return marine_variables[None]


def solution(mesh):
    placed = (
        P("dom", None, None, "gx", "gy"),
        P(None, "gx", "gy"),
        P("dom", None, "gx", "gy"),
        P(),
    )
    return jax.shard_map(
        per_device,
        mesh=mesh,
        in_specs=placed,
        out_specs=P("dom", None, None, "gx", "gy"),
        check_vma=False,
    )
```

```python
import jax
import jax.numpy as jnp
from jax import lax
from jax.sharding import PartitionSpec as P

STEPS = 4
TILE = 8


ADVECT = 0.2
DIFFUSE = 0.15
BUOY_TEMP = 0.2
BUOY_SALT = 0.1
PRESS_SCALE = 0.25
WIND_SCALE = 0.2
CORIO_BASE = 0.1
CORIO_SLOPE = 0.1


def shift_pairs(axis, wrap):
    size = lax.axis_size(axis)
    up = [(i, (i + 1) % size) for i in range(size if wrap else size - 1)]
    return up, [(j, i) for i, j in up]


def with_halo(x):
    x_up, x_down = shift_pairs("gx", True)
    y_up, y_down = shift_pairs("gy", False)
    west = lax.ppermute(x[:, :, -1:, :], "gx", x_up)
    east = lax.ppermute(x[:, :, :1, :], "gx", x_down)
    south = lax.ppermute(x[:, :, :, -1:], "gy", y_up)
    north = lax.ppermute(x[:, :, :, :1], "gy", y_down)
    wide = jnp.concatenate([west, x, east], axis=2)
    corner = ((0, 0), (0, 0), (1, 1), (0, 0))
    return jnp.concatenate(
        [jnp.pad(south, corner), wide, jnp.pad(north, corner)], axis=3
    )


def advance(padded, topmost_slab, eddy_diffusivity, coriolis):
    centre = padded[:, :, 1:-1, 1:-1]
    eastern_neighbour_cell = padded[:, :, 2:, 1:-1]
    west_cell = padded[:, :, :-2, 1:-1]
    north_cell = padded[:, :, 1:-1, 2:]
    south_cell = padded[:, :, 1:-1, :-2]
    grad_x = 0.5 * (eastern_neighbour_cell - west_cell)
    grad_y = 0.5 * (north_cell - south_cell)
    spread = eastern_neighbour_cell + west_cell + north_cell + south_cell - 4.0 * centre
    buoyancy = BUOY_TEMP * padded[2] - BUOY_SALT * padded[3]
    pressure = PRESS_SCALE * jnp.cumsum(buoyancy, axis=0)
    press_x = 0.5 * (pressure[:, 2:, 1:-1] - pressure[:, :-2, 1:-1])
    press_y = 0.5 * (pressure[:, 1:-1, 2:] - pressure[:, 1:-1, :-2])
    vert_flux = eddy_diffusivity[None, :, None, None] * (centre[:, 1:] - centre[:, :-1])
    closed = jnp.zeros_like(centre[:, :1])
    vertical = jnp.concatenate([vert_flux, closed], axis=1) - jnp.concatenate(
        [closed, vert_flux], axis=1
    )
    east_vel = centre[0]
    north_vel = centre[1]
    carried_over = east_vel[None] * grad_x + north_vel[None] * grad_y
    common = centre - ADVECT * carried_over + DIFFUSE * spread + vertical
    level_top = (jnp.arange(centre.shape[1]) == 0).astype(jnp.float32)[:, None, None]
    forcing = WIND_SCALE * topmost_slab[:, None] * level_top
    east_next = common[0] + coriolis * north_vel - press_x + forcing[0]
    north_next = common[1] - coriolis * east_vel - press_y + forcing[1]
    return jnp.stack([east_next, north_next, common[2], common[3]])


def coriolis_at(positions, total_rows):
    return CORIO_BASE + CORIO_SLOPE * (positions.astype(jnp.float32) + 0.5) / total_rows


def resample(ensemble, ancestors):
    members = lax.axis_size("dom")
    block = ensemble[0]
    fields, levels, width_x, width_y = block.shape
    groups = fields * levels // members
    parts = block.reshape(members, groups, width_x, width_y)
    by_member = lax.all_to_all(parts, "dom", 0, 0, tiled=True)
    tiles = ancestors[:, 0, :]
    cell_source = jnp.repeat(tiles, TILE, 1)[:, None, None, :]
    picked = jnp.zeros_like(by_member)
    for member in range(members):
        picked = jnp.where(cell_source == member, by_member[member][None], picked)
    back = lax.all_to_all(picked, "dom", 0, 0, tiled=True)
    return back.reshape(fields, levels, width_x, width_y)


def per_device(ensemble, ancestors, particle_air_drag, eddy_diffusivity):
    width_y = ensemble.shape[4]
    selected_particles = resample(ensemble, ancestors)
    row_block = lax.axis_index("gy")
    total_rows = width_y * lax.axis_size("gy")
    topmost_slab = particle_air_drag[0]
    positions = row_block * width_y + jnp.arange(width_y, dtype=jnp.int32)
    coriolis = coriolis_at(positions, total_rows)
    marine_variables = selected_particles
    for iteration in range(STEPS):
        padded = with_halo(marine_variables)
        marine_variables = advance(padded, topmost_slab, eddy_diffusivity, coriolis)
    return marine_variables[None]


def solution(mesh):
    placed = (
        P("dom", None, None, "gx", "gy"),
        P(None, "gx", "gy"),
        P("dom", None, "gx", "gy"),
        P(),
    )
    return jax.shard_map(
        per_device,
        mesh=mesh,
        in_specs=placed,
        out_specs=P("dom", None, None, "gx", "gy"),
        check_vma=False,
    )
```

```python
import jax
import jax.numpy as jnp
from jax import lax
from jax.sharding import PartitionSpec as P
from jax.experimental import pallas as pl
from jax.experimental.pallas import tpu as pltpu

STEPS = 4
TILE = 8


ADVECT = 0.2
DIFFUSE = 0.15
BUOY_TEMP = 0.2
BUOY_SALT = 0.1
PRESS_SCALE = 0.25
WIND_SCALE = 0.2
CORIO_BASE = 0.1
CORIO_SLOPE = 0.1


HALO = STEPS


def shift_pairs(axis, wrap):
    size = lax.axis_size(axis)
    up = [(i, (i + 1) % size) for i in range(size if wrap else size - 1)]
    return up, [(j, i) for i, j in up]


def with_wide_halo(packed, lanes):
    x_up, x_down = shift_pairs("gx", True)
    width_x = packed.shape[1]
    west = lax.ppermute(packed[:, width_x - HALO:, :], "gx", x_up)
    east = lax.ppermute(packed[:, :HALO, :], "gx", x_down)
    rows = jnp.concatenate([packed, east, west], axis=1)
    y_up, y_down = shift_pairs("gy", False)
    width_y = rows.shape[2]
    south = lax.ppermute(rows[:, :, width_y - HALO:], "gy", y_up)
    north = lax.ppermute(rows[:, :, :HALO], "gy", y_down)
    gap = jnp.zeros(rows.shape[:2] + (lanes - width_y - 2 * HALO,), rows.dtype)
    return jnp.concatenate([rows, north, gap, south], axis=2)


def forecast_kernel(levels, eddy_ref, cor_ref, mask_ref, full_ref, out_ref, buf0, buf1):
    cor = cor_ref[...]
    inside = mask_ref[...] > 0.5
    rows, lanes = full_ref.shape[1], full_ref.shape[2]
    state_rows = 4 * levels
    drag0 = WIND_SCALE * full_ref[state_rows]
    drag1 = WIND_SCALE * full_ref[state_rows + 1]

    def around(a):
        return (
            pltpu.roll(a, rows - 1, 0),
            pltpu.roll(a, 1, 0),
            pltpu.roll(a, lanes - 1, 1),
            pltpu.roll(a, 1, 1),
        )

    def one_step(src, dst, last):
        def level(k, total):
            above = jnp.minimum(k + 1, levels - 1)
            below = jnp.maximum(k - 1, 0)
            c = [src[f * levels + k] for f in range(4)]
            up = [src[f * levels + above] for f in range(4)]
            dn = [src[f * levels + below] for f in range(4)]
            e_up = eddy_ref[k + 1]
            e_dn = eddy_ref[k]
            total = total + (BUOY_TEMP * c[2] - BUOY_SALT * c[3])
            pressure = PRESS_SCALE * total
            east_vel, north_vel = c[0], c[1]
            new = []
            for f in range(4):
                e, w, n, s = around(c[f])
                grad_x = 0.5 * (e - w)
                grad_y = 0.5 * (n - s)
                spread = e + w + n + s - 4.0 * c[f]
                vertical = e_up * (up[f] - c[f]) - e_dn * (c[f] - dn[f])
                carried = east_vel * grad_x + north_vel * grad_y
                new.append(c[f] - ADVECT * carried + DIFFUSE * spread + vertical)
            pe, pw, pn, ps = around(pressure)
            top = jnp.where(k == 0, 1.0, 0.0).astype(jnp.float32)
            new[0] = new[0] + cor * north_vel - 0.5 * (pe - pw) + drag0 * top
            new[1] = new[1] - cor * east_vel - 0.5 * (pn - ps) + drag1 * top
            for f in range(4):
                if last:
                    out_ref[f * levels + k] = new[f][: out_ref.shape[1], : out_ref.shape[2]]
                else:
                    dst[f * levels + k] = jnp.where(inside, new[f], 0.0)
            return total

        lax.fori_loop(0, levels, level, jnp.zeros((rows, lanes), jnp.float32))

    bufs = (buf0, buf1)
    src = full_ref
    for step in range(STEPS):
        dst = bufs[step % 2]
        one_step(src, dst, step == STEPS - 1)
        src = dst


def forecast(full, eddy, cor, inside, levels, width_x, width_y):
    state_rows, rows, lanes = 4 * levels, full.shape[1], full.shape[2]
    kernel = lambda *refs: forecast_kernel(levels, *refs)
    vmem = pl.BlockSpec(memory_space=pltpu.VMEM)
    cells = state_rows * rows * lanes
    return pl.pallas_call(
        kernel,
        out_shape=jax.ShapeDtypeStruct((state_rows, width_x, width_y), jnp.float32),
        in_specs=[pl.BlockSpec(memory_space=pltpu.SMEM), vmem, vmem, vmem],
        out_specs=vmem,
        scratch_shapes=[pltpu.VMEM((state_rows, rows, lanes), jnp.float32)] * 2,
        cost_estimate=pl.CostEstimate(
            flops=STEPS * cells * 40, transcendentals=0, bytes_accessed=full.size * 4 + state_rows * width_x * width_y * 4
        ),
    )(eddy, cor, inside, full)


def coriolis_at(positions, total_rows):
    return CORIO_BASE + CORIO_SLOPE * (positions.astype(jnp.float32) + 0.5) / total_rows


def resample(ensemble, ancestors):
    members = lax.axis_size("dom")
    block = ensemble[0]
    fields, levels, width_x, width_y = block.shape
    groups = fields * levels // members
    parts = block.reshape(members, groups, width_x, width_y)
    by_member = lax.all_to_all(parts, "dom", 0, 0, tiled=True)
    tiles = ancestors[:, 0, :]
    cell_source = jnp.repeat(tiles, TILE, 1)[:, None, None, :]
    picked = jnp.zeros_like(by_member)
    for member in range(members):
        picked = jnp.where(cell_source == member, by_member[member][None], picked)
    back = lax.all_to_all(picked, "dom", 0, 0, tiled=True)
    return back.reshape(fields, levels, width_x, width_y)


def per_device(ensemble, ancestors, particle_air_drag, eddy_diffusivity):
    _, fields, levels, width_x, width_y = ensemble.shape
    selected = resample(ensemble, ancestors)
    packed = jnp.concatenate(
        [selected.reshape(fields * levels, width_x, width_y), particle_air_drag[0]], axis=0
    )
    lanes = 2 * width_y
    full = with_wide_halo(packed, lanes)
    lane = jnp.arange(lanes, dtype=jnp.int32)
    offset = jnp.where(lane < width_y + 2 * HALO + (lanes - width_y - 2 * HALO) // 2, lane, lane - lanes)
    row_block = lax.axis_index("gy")
    total_rows = width_y * lax.axis_size("gy")
    positions = row_block * width_y + offset
    cor = coriolis_at(positions, total_rows)[None]
    used = (offset < width_y + HALO) & (offset >= -HALO)
    inside = (used & (positions >= 0) & (positions < total_rows)).astype(jnp.float32)[None]
    zero = jnp.zeros((1,), jnp.float32)
    eddy = jnp.concatenate([zero, eddy_diffusivity, zero])
    out = forecast(full, eddy, cor, inside, levels, width_x, width_y)
    return out.reshape(1, fields, levels, width_x, width_y)


def solution(mesh):
    placed = (
        P("dom", None, None, "gx", "gy"),
        P(None, "gx", "gy"),
        P("dom", None, "gx", "gy"),
        P(),
    )
    return jax.shard_map(
        per_device,
        mesh=mesh,
        in_specs=placed,
        out_specs=P("dom", None, None, "gx", "gy"),
        check_vma=False,
    )
```

```python
import jax
import jax.numpy as jnp
from jax import lax
from jax.sharding import PartitionSpec as P
from jax.experimental import pallas as pl
from jax.experimental.pallas import tpu as pltpu

STEPS = 4
TILE = 8


ADVECT = 0.2
DIFFUSE = 0.15
BUOY_TEMP = 0.2
BUOY_SALT = 0.1
PRESS_SCALE = 0.25
WIND_SCALE = 0.2
CORIO_BASE = 0.1
CORIO_SLOPE = 0.1


HALO = STEPS


def shift_pairs(axis, wrap):
    size = lax.axis_size(axis)
    up = [(i, (i + 1) % size) for i in range(size if wrap else size - 1)]
    return up, [(j, i) for i, j in up]


def halo_pieces(packed):
    x_up, x_down = shift_pairs("gx", True)
    width_x = packed.shape[1]
    west = lax.ppermute(packed[:, width_x - HALO:, :], "gx", x_up)
    east = lax.ppermute(packed[:, :HALO, :], "gx", x_down)
    rows = jnp.concatenate([packed, east, west], axis=1)
    y_up, y_down = shift_pairs("gy", False)
    width_y = rows.shape[2]
    south = lax.ppermute(rows[:, :, width_y - HALO:], "gy", y_up)
    north = lax.ppermute(rows[:, :, :HALO], "gy", y_down)
    return east, west, north, south


def forecast_kernel(levels, eddy_ref, cor_ref, mask_ref, centre_ref, east_ref,
                    west_ref, north_ref, south_ref, out_ref, buf0, buf1):
    n_rows, lanes = buf0.shape[1], buf0.shape[2]
    wx, wy = centre_ref.shape[1], centre_ref.shape[2]
    buf0[:, :wx, :wy] = centre_ref[...]
    buf0[:, wx:wx + HALO, :wy] = east_ref[...]
    buf0[:, wx + HALO:, :wy] = west_ref[...]
    buf0[:, :, wy:] = jnp.zeros((buf0.shape[0], n_rows, lanes - wy), jnp.float32)
    buf0[:, :, wy:wy + HALO] = north_ref[...]
    buf0[:, :, lanes - HALO:] = south_ref[...]

    cor = cor_ref[...]
    inside = mask_ref[...] > 0.5
    state_rows = 4 * levels
    drag = [WIND_SCALE * buf0[state_rows + i] for i in range(2)]

    def around(a):
        return (
            pltpu.roll(a, n_rows - 1, 0),
            pltpu.roll(a, 1, 0),
            pltpu.roll(a, lanes - 1, 1),
            pltpu.roll(a, 1, 1),
        )

    row8 = lax.broadcasted_iota(jnp.int32, (wx, wy), 0)
    lane8 = lax.broadcasted_iota(jnp.int32, (wx, wy), 1)

    def around_block(lo, nx, hi):
        return (
            jnp.where(row8 == wx - 1, pltpu.roll(nx, wx - 1, 0), pltpu.roll(lo, wx - 1, 0)),
            jnp.where(row8 == 0, pltpu.roll(nx, 1, 0), pltpu.roll(lo, 1, 0)),
            jnp.where(lane8 == wy - 1, pltpu.roll(hi, wy - 1, 1), pltpu.roll(lo, wy - 1, 1)),
            jnp.where(lane8 == 0, pltpu.roll(hi, 1, 1), pltpu.roll(lo, 1, 1)),
        )

    def tendencies(k, c, up, dn, nb, total, nbt, cor_k, drag_k):
        e_up = eddy_ref[k + 1]
        e_dn = eddy_ref[k]
        east_vel, north_vel = c[0], c[1]
        new = []
        for f in range(4):
            e, w, n, s = nb[f]
            spread = e + w + n + s - 4.0 * c[f]
            vertical = e_up * (up[f] - c[f]) - e_dn * (c[f] - dn[f])
            carried = east_vel * (e - w) + north_vel * (n - s)
            new.append(c[f] - (0.5 * ADVECT) * carried + DIFFUSE * spread + vertical)
        pe, pw, pn, ps = nbt
        top = jnp.where(k == 0, 1.0, 0.0).astype(jnp.float32)
        new[0] = new[0] + cor_k * north_vel - (0.5 * PRESS_SCALE) * (pe - pw) + drag_k[0] * top
        new[1] = new[1] - cor_k * east_vel - (0.5 * PRESS_SCALE) * (pn - ps) + drag_k[1] * top
        return new

    def one_step(src, dst):
        def level(k, total):
            above = jnp.minimum(k + 1, levels - 1)
            below = jnp.maximum(k - 1, 0)
            c = [src[f * levels + k] for f in range(4)]
            up = [src[f * levels + above] for f in range(4)]
            dn = [src[f * levels + below] for f in range(4)]
            total = total + (BUOY_TEMP * c[2] - BUOY_SALT * c[3])
            nb = [around(c[f]) for f in range(4)]
            new = tendencies(k, c, up, dn, nb, total, around(total), cor, drag)
            for f in range(4):
                dst[f * levels + k] = jnp.where(inside, new[f], 0.0)
            return total

        lax.fori_loop(0, levels, level, jnp.zeros((n_rows, lanes), jnp.float32))

    def last_step(src):
        def pieces(i):
            return (src[i, :wx, :wy], src[i, wx:, :wy], src[i, :wx, wy:])

        drag_b = [d[:wx, :wy] for d in drag]
        cor_b = cor[:, :wy]

        def level(k, totals):
            above = jnp.minimum(k + 1, levels - 1)
            below = jnp.maximum(k - 1, 0)
            cp = [pieces(f * levels + k) for f in range(4)]
            c = [p[0] for p in cp]
            up = [src[f * levels + above, :wx, :wy] for f in range(4)]
            dn = [src[f * levels + below, :wx, :wy] for f in range(4)]
            totals = tuple(
                t + (BUOY_TEMP * a - BUOY_SALT * b) for t, a, b in zip(totals, cp[2], cp[3])
            )
            nb = [around_block(*p) for p in cp]
            new = tendencies(k, c, up, dn, nb, totals[0], around_block(*totals), cor_b, drag_b)
            for f in range(4):
                out_ref[f * levels + k] = new[f]
            return totals

        zero = jnp.zeros((wx, wy), jnp.float32)
        lax.fori_loop(0, levels, level, (zero, zero, zero))

    one_step(buf0, buf1)
    one_step(buf1, buf0)
    one_step(buf0, buf1)
    last_step(buf1)


def forecast(pieces, eddy, cor, inside, levels):
    centre = pieces[0]
    packed_rows, width_x, width_y = centre.shape
    state_rows = 4 * levels
    rows, lanes = width_x + 2 * HALO, 2 * width_y
    kernel = lambda *refs: forecast_kernel(levels, *refs)
    vmem = pl.BlockSpec(memory_space=pltpu.VMEM)
    cells = state_rows * rows * lanes
    return pl.pallas_call(
        kernel,
        out_shape=jax.ShapeDtypeStruct((state_rows, width_x, width_y), jnp.float32),
        in_specs=[pl.BlockSpec(memory_space=pltpu.SMEM)] + [vmem] * 7,
        out_specs=vmem,
        scratch_shapes=[
            pltpu.VMEM((packed_rows, rows, lanes), jnp.float32),
            pltpu.VMEM((state_rows, rows, lanes), jnp.float32),
        ],
        cost_estimate=pl.CostEstimate(
            flops=STEPS * cells * 40, transcendentals=0,
            bytes_accessed=2 * centre.size * 4 + state_rows * width_x * width_y * 4,
        ),
    )(eddy, cor, inside, *pieces)


def coriolis_at(positions, total_rows):
    return CORIO_BASE + CORIO_SLOPE * (positions.astype(jnp.float32) + 0.5) / total_rows


def resample(ensemble, ancestors):
    members = lax.axis_size("dom")
    block = ensemble[0]
    fields, levels, width_x, width_y = block.shape
    groups = fields * levels // members
    parts = block.reshape(members, groups, width_x, width_y)
    by_member = lax.all_to_all(parts, "dom", 0, 0, tiled=True)
    tiles = ancestors[:, 0, :]
    cell_source = jnp.repeat(tiles, TILE, 1)[:, None, None, :]
    picked = jnp.zeros_like(by_member)
    for member in range(members):
        picked = jnp.where(cell_source == member, by_member[member][None], picked)
    back = lax.all_to_all(picked, "dom", 0, 0, tiled=True)
    return back.reshape(fields, levels, width_x, width_y)


def per_device(ensemble, ancestors, particle_air_drag, eddy_diffusivity):
    _, fields, levels, width_x, width_y = ensemble.shape
    selected = resample(ensemble, ancestors)
    packed = jnp.concatenate(
        [selected.reshape(fields * levels, width_x, width_y), particle_air_drag[0]], axis=0
    )
    lanes = 2 * width_y
    pieces = (packed,) + halo_pieces(packed)
    lane = jnp.arange(lanes, dtype=jnp.int32)
    offset = jnp.where(lane < width_y + 2 * HALO + (lanes - width_y - 2 * HALO) // 2, lane, lane - lanes)
    row_block = lax.axis_index("gy")
    total_rows = width_y * lax.axis_size("gy")
    positions = row_block * width_y + offset
    cor = coriolis_at(positions, total_rows)[None]
    used = (offset < width_y + HALO) & (offset >= -HALO)
    inside = (used & (positions >= 0) & (positions < total_rows)).astype(jnp.float32)[None]
    zero = jnp.zeros((1,), jnp.float32)
    eddy = jnp.concatenate([zero, eddy_diffusivity, zero])
    out = forecast(pieces, eddy, cor, inside, levels)
    return out.reshape(1, fields, levels, width_x, width_y)


def solution(mesh):
    placed = (
        P("dom", None, None, "gx", "gy"),
        P(None, "gx", "gy"),
        P("dom", None, "gx", "gy"),
        P(),
    )
    return jax.shard_map(
        per_device,
        mesh=mesh,
        in_specs=placed,
        out_specs=P("dom", None, None, "gx", "gy"),
        check_vma=False,
    )
```

```python
import jax
import jax.numpy as jnp
from jax import lax
from jax.sharding import PartitionSpec as P
from jax.experimental import pallas as pl
from jax.experimental.pallas import tpu as pltpu

STEPS = 4
TILE = 8


ADVECT = 0.2
DIFFUSE = 0.15
BUOY_TEMP = 0.2
BUOY_SALT = 0.1
PRESS_SCALE = 0.25
WIND_SCALE = 0.2
CORIO_BASE = 0.1
CORIO_SLOPE = 0.1


HALO = STEPS


def shift_pairs(axis, wrap):
    size = lax.axis_size(axis)
    up = [(i, (i + 1) % size) for i in range(size if wrap else size - 1)]
    return up, [(j, i) for i, j in up]


def with_wide_halo(packed, lanes):
    x_up, x_down = shift_pairs("gx", True)
    width_x = packed.shape[1]
    west = lax.ppermute(packed[:, width_x - HALO:, :], "gx", x_up)
    east = lax.ppermute(packed[:, :HALO, :], "gx", x_down)
    rows = jnp.concatenate([packed, east, west], axis=1)
    y_up, y_down = shift_pairs("gy", False)
    width_y = rows.shape[2]
    south = lax.ppermute(rows[:, :, width_y - HALO:], "gy", y_up)
    north = lax.ppermute(rows[:, :, :HALO], "gy", y_down)
    gap = jnp.zeros(rows.shape[:2] + (lanes - width_y - 2 * HALO,), rows.dtype)
    return jnp.concatenate([rows, north, gap, south], axis=2)


def forecast_kernel(levels, eddy_ref, cor_ref, mask_ref, full_ref, out_ref, buf0, buf1):
    n_rows, lanes = full_ref.shape[1], full_ref.shape[2]
    wx, wy = out_ref.shape[1], out_ref.shape[2]

    cor = cor_ref[...]
    inside = mask_ref[...] > 0.5
    state_rows = 4 * levels
    drag = [WIND_SCALE * full_ref[state_rows + i] for i in range(2)]

    def around(a):
        return (
            pltpu.roll(a, n_rows - 1, 0),
            pltpu.roll(a, 1, 0),
            pltpu.roll(a, lanes - 1, 1),
            pltpu.roll(a, 1, 1),
        )

    row8 = lax.broadcasted_iota(jnp.int32, (wx, wy), 0)
    lane8 = lax.broadcasted_iota(jnp.int32, (wx, wy), 1)

    def around_block(lo, nx, hi):
        return (
            jnp.where(row8 == wx - 1, pltpu.roll(nx, wx - 1, 0), pltpu.roll(lo, wx - 1, 0)),
            jnp.where(row8 == 0, pltpu.roll(nx, 1, 0), pltpu.roll(lo, 1, 0)),
            jnp.where(lane8 == wy - 1, pltpu.roll(hi, wy - 1, 1), pltpu.roll(lo, wy - 1, 1)),
            jnp.where(lane8 == 0, pltpu.roll(hi, 1, 1), pltpu.roll(lo, 1, 1)),
        )

    def tendencies(k, c, up, dn, nb, total, nbt, cor_k, drag_k):
        e_up = eddy_ref[k + 1]
        e_dn = eddy_ref[k]
        east_vel, north_vel = c[0], c[1]
        new = []
        for f in range(4):
            e, w, n, s = nb[f]
            spread = e + w + n + s - 4.0 * c[f]
            vertical = e_up * (up[f] - c[f]) - e_dn * (c[f] - dn[f])
            carried = east_vel * (e - w) + north_vel * (n - s)
            new.append(c[f] - (0.5 * ADVECT) * carried + DIFFUSE * spread + vertical)
        pe, pw, pn, ps = nbt
        top = jnp.where(k == 0, 1.0, 0.0).astype(jnp.float32)
        new[0] = new[0] + cor_k * north_vel - (0.5 * PRESS_SCALE) * (pe - pw) + drag_k[0] * top
        new[1] = new[1] - cor_k * east_vel - (0.5 * PRESS_SCALE) * (pn - ps) + drag_k[1] * top
        return new

    def one_step(src, dst):
        def level(k, total):
            above = jnp.minimum(k + 1, levels - 1)
            below = jnp.maximum(k - 1, 0)
            c = [src[f * levels + k] for f in range(4)]
            up = [src[f * levels + above] for f in range(4)]
            dn = [src[f * levels + below] for f in range(4)]
            total = total + (BUOY_TEMP * c[2] - BUOY_SALT * c[3])
            nb = [around(c[f]) for f in range(4)]
            new = tendencies(k, c, up, dn, nb, total, around(total), cor, drag)
            for f in range(4):
                dst[f * levels + k] = jnp.where(inside, new[f], 0.0)
            return total

        lax.fori_loop(0, levels, level, jnp.zeros((n_rows, lanes), jnp.float32))

    def last_step(src):
        def pieces(i):
            return (src[i, :wx, :wy], src[i, wx:, :wy], src[i, :wx, wy:])

        drag_b = [d[:wx, :wy] for d in drag]
        cor_b = cor[:, :wy]

        def level(k, totals):
            above = jnp.minimum(k + 1, levels - 1)
            below = jnp.maximum(k - 1, 0)
            cp = [pieces(f * levels + k) for f in range(4)]
            c = [p[0] for p in cp]
            up = [src[f * levels + above, :wx, :wy] for f in range(4)]
            dn = [src[f * levels + below, :wx, :wy] for f in range(4)]
            totals = tuple(
                t + (BUOY_TEMP * a - BUOY_SALT * b) for t, a, b in zip(totals, cp[2], cp[3])
            )
            nb = [around_block(*p) for p in cp]
            new = tendencies(k, c, up, dn, nb, totals[0], around_block(*totals), cor_b, drag_b)
            for f in range(4):
                out_ref[f * levels + k] = new[f]
            return totals

        zero = jnp.zeros((wx, wy), jnp.float32)
        lax.fori_loop(0, levels, level, (zero, zero, zero))

    one_step(full_ref, buf1)
    one_step(buf1, buf0)
    one_step(buf0, buf1)
    last_step(buf1)


def forecast(full, eddy, cor, inside, levels, width_x, width_y):
    state_rows, rows, lanes = 4 * levels, full.shape[1], full.shape[2]
    kernel = lambda *refs: forecast_kernel(levels, *refs)
    vmem = pl.BlockSpec(memory_space=pltpu.VMEM)
    cells = state_rows * rows * lanes
    return pl.pallas_call(
        kernel,
        out_shape=jax.ShapeDtypeStruct((state_rows, width_x, width_y), jnp.float32),
        in_specs=[pl.BlockSpec(memory_space=pltpu.SMEM), vmem, vmem, vmem],
        out_specs=vmem,
        scratch_shapes=[pltpu.VMEM((state_rows, rows, lanes), jnp.float32)] * 2,
        cost_estimate=pl.CostEstimate(
            flops=STEPS * cells * 40, transcendentals=0,
            bytes_accessed=full.size * 4 + state_rows * width_x * width_y * 4,
        ),
    )(eddy, cor, inside, full)


def coriolis_at(positions, total_rows):
    return CORIO_BASE + CORIO_SLOPE * (positions.astype(jnp.float32) + 0.5) / total_rows


def resample(ensemble, ancestors):
    members = lax.axis_size("dom")
    block = ensemble[0]
    fields, levels, width_x, width_y = block.shape
    groups = fields * levels // members
    parts = block.reshape(members, groups, width_x, width_y)
    by_member = lax.all_to_all(parts, "dom", 0, 0, tiled=True)
    tiles = ancestors[:, 0, :]
    cell_source = jnp.repeat(tiles, TILE, 1)[:, None, None, :]
    picked = jnp.zeros_like(by_member)
    for member in range(members):
        picked = jnp.where(cell_source == member, by_member[member][None], picked)
    back = lax.all_to_all(picked, "dom", 0, 0, tiled=True)
    return back.reshape(fields, levels, width_x, width_y)


def per_device(ensemble, ancestors, particle_air_drag, eddy_diffusivity):
    _, fields, levels, width_x, width_y = ensemble.shape
    selected = resample(ensemble, ancestors)
    packed = jnp.concatenate(
        [selected.reshape(fields * levels, width_x, width_y), particle_air_drag[0]], axis=0
    )
    lanes = 2 * width_y
    full = with_wide_halo(packed, lanes)
    lane = jnp.arange(lanes, dtype=jnp.int32)
    offset = jnp.where(lane < width_y + 2 * HALO + (lanes - width_y - 2 * HALO) // 2, lane, lane - lanes)
    row_block = lax.axis_index("gy")
    total_rows = width_y * lax.axis_size("gy")
    positions = row_block * width_y + offset
    cor = coriolis_at(positions, total_rows)[None]
    used = (offset < width_y + HALO) & (offset >= -HALO)
    inside = (used & (positions >= 0) & (positions < total_rows)).astype(jnp.float32)[None]
    zero = jnp.zeros((1,), jnp.float32)
    eddy = jnp.concatenate([zero, eddy_diffusivity, zero])
    out = forecast(full, eddy, cor, inside, levels, width_x, width_y)
    return out.reshape(1, fields, levels, width_x, width_y)


def solution(mesh):
    placed = (
        P("dom", None, None, "gx", "gy"),
        P(None, "gx", "gy"),
        P("dom", None, "gx", "gy"),
        P(),
    )
    return jax.shard_map(
        per_device,
        mesh=mesh,
        in_specs=placed,
        out_specs=P("dom", None, None, "gx", "gy"),
        check_vma=False,
    )
```

```python
import jax
import jax.numpy as jnp
from jax import lax
from jax.sharding import PartitionSpec as P
from jax.experimental import pallas as pl
from jax.experimental.pallas import tpu as pltpu

STEPS = 4
TILE = 8


ADVECT = 0.2
DIFFUSE = 0.15
BUOY_TEMP = 0.2
BUOY_SALT = 0.1
PRESS_SCALE = 0.25
WIND_SCALE = 0.2
CORIO_BASE = 0.1
CORIO_SLOPE = 0.1


HALO = STEPS


def shift_pairs(axis, wrap):
    size = lax.axis_size(axis)
    up = [(i, (i + 1) % size) for i in range(size if wrap else size - 1)]
    return up, [(j, i) for i, j in up]


def with_wide_halo(packed, lanes):
    x_up, x_down = shift_pairs("gx", True)
    width_x = packed.shape[1]
    west = lax.ppermute(packed[:, width_x - HALO:, :], "gx", x_up)
    east = lax.ppermute(packed[:, :HALO, :], "gx", x_down)
    rows = jnp.concatenate([packed, east, west], axis=1)
    y_up, y_down = shift_pairs("gy", False)
    width_y = rows.shape[2]
    south = lax.ppermute(rows[:, :, width_y - HALO:], "gy", y_up)
    north = lax.ppermute(rows[:, :, :HALO], "gy", y_down)
    gap = jnp.zeros(rows.shape[:2] + (lanes - width_y - 2 * HALO,), rows.dtype)
    return jnp.concatenate([rows, north, gap, south], axis=2)


def forecast_kernel(levels, eddy_ref, cor_ref, mask_ref, full_ref, out_ref, buf0, buf1):
    n_rows, lanes = full_ref.shape[1], full_ref.shape[2]
    wx, wy = out_ref.shape[1], out_ref.shape[2]

    cor = cor_ref[...]
    inside = mask_ref[...] > 0.5
    state_rows = 4 * levels
    drag = [WIND_SCALE * full_ref[state_rows + i] for i in range(2)]

    def around(a):
        return (
            pltpu.roll(a, n_rows - 1, 0),
            pltpu.roll(a, 1, 0),
            pltpu.roll(a, lanes - 1, 1),
            pltpu.roll(a, 1, 1),
        )

    row8 = lax.broadcasted_iota(jnp.int32, (wx, wy), 0)
    lane8 = lax.broadcasted_iota(jnp.int32, (wx, wy), 1)

    def around_block(lo, nx, hi):
        return (
            jnp.where(row8 == wx - 1, pltpu.roll(nx, wx - 1, 0), pltpu.roll(lo, wx - 1, 0)),
            jnp.where(row8 == 0, pltpu.roll(nx, 1, 0), pltpu.roll(lo, 1, 0)),
            jnp.where(lane8 == wy - 1, pltpu.roll(hi, wy - 1, 1), pltpu.roll(lo, wy - 1, 1)),
            jnp.where(lane8 == 0, pltpu.roll(hi, 1, 1), pltpu.roll(lo, 1, 1)),
        )

    def tendencies(k, c, up, dn, nb, total, nbt, cor_k, drag_k):
        e_up = eddy_ref[k + 1]
        e_dn = eddy_ref[k]
        east_vel, north_vel = c[0], c[1]
        new = []
        for f in range(4):
            e, w, n, s = nb[f]
            spread = e + w + n + s - 4.0 * c[f]
            vertical = e_up * (up[f] - c[f]) - e_dn * (c[f] - dn[f])
            carried = east_vel * (e - w) + north_vel * (n - s)
            new.append(c[f] - (0.5 * ADVECT) * carried + DIFFUSE * spread + vertical)
        pe, pw, pn, ps = nbt
        top = jnp.where(k == 0, 1.0, 0.0).astype(jnp.float32)
        new[0] = new[0] + cor_k * north_vel - (0.5 * PRESS_SCALE) * (pe - pw) + drag_k[0] * top
        new[1] = new[1] - cor_k * east_vel - (0.5 * PRESS_SCALE) * (pn - ps) + drag_k[1] * top
        return new

    def one_step(src, dst):
        def level(k, total):
            above = jnp.minimum(k + 1, levels - 1)
            below = jnp.maximum(k - 1, 0)
            c = [src[f * levels + k] for f in range(4)]
            up = [src[f * levels + above] for f in range(4)]
            dn = [src[f * levels + below] for f in range(4)]
            total = total + (BUOY_TEMP * c[2] - BUOY_SALT * c[3])
            nb = [around(c[f]) for f in range(4)]
            new = tendencies(k, c, up, dn, nb, total, around(total), cor, drag)
            for f in range(4):
                dst[f * levels + k] = jnp.where(inside, new[f], 0.0)
            return total

        lax.fori_loop(0, levels, level, jnp.zeros((n_rows, lanes), jnp.float32), unroll=True)

    def last_step(src):
        def pieces(i):
            return (src[i, :wx, :wy], src[i, wx:, :wy], src[i, :wx, wy:])

        drag_b = [d[:wx, :wy] for d in drag]
        cor_b = cor[:, :wy]

        def level(k, totals):
            above = jnp.minimum(k + 1, levels - 1)
            below = jnp.maximum(k - 1, 0)
            cp = [pieces(f * levels + k) for f in range(4)]
            c = [p[0] for p in cp]
            up = [src[f * levels + above, :wx, :wy] for f in range(4)]
            dn = [src[f * levels + below, :wx, :wy] for f in range(4)]
            totals = tuple(
                t + (BUOY_TEMP * a - BUOY_SALT * b) for t, a, b in zip(totals, cp[2], cp[3])
            )
            nb = [around_block(*p) for p in cp]
            new = tendencies(k, c, up, dn, nb, totals[0], around_block(*totals), cor_b, drag_b)
            for f in range(4):
                out_ref[f * levels + k] = new[f]
            return totals

        zero = jnp.zeros((wx, wy), jnp.float32)
        lax.fori_loop(0, levels, level, (zero, zero, zero), unroll=True)

    one_step(full_ref, buf1)
    one_step(buf1, buf0)
    one_step(buf0, buf1)
    last_step(buf1)


def forecast(full, eddy, cor, inside, levels, width_x, width_y):
    state_rows, rows, lanes = 4 * levels, full.shape[1], full.shape[2]
    kernel = lambda *refs: forecast_kernel(levels, *refs)
    vmem = pl.BlockSpec(memory_space=pltpu.VMEM)
    cells = state_rows * rows * lanes
    return pl.pallas_call(
        kernel,
        out_shape=jax.ShapeDtypeStruct((state_rows, width_x, width_y), jnp.float32),
        in_specs=[pl.BlockSpec(memory_space=pltpu.SMEM), vmem, vmem, vmem],
        out_specs=vmem,
        scratch_shapes=[pltpu.VMEM((state_rows, rows, lanes), jnp.float32)] * 2,
        cost_estimate=pl.CostEstimate(
            flops=STEPS * cells * 40, transcendentals=0,
            bytes_accessed=full.size * 4 + state_rows * width_x * width_y * 4,
        ),
    )(eddy, cor, inside, full)


def coriolis_at(positions, total_rows):
    return CORIO_BASE + CORIO_SLOPE * (positions.astype(jnp.float32) + 0.5) / total_rows


def resample(ensemble, ancestors):
    members = lax.axis_size("dom")
    block = ensemble[0]
    fields, levels, width_x, width_y = block.shape
    groups = fields * levels // members
    parts = block.reshape(members, groups, width_x, width_y)
    by_member = lax.all_to_all(parts, "dom", 0, 0, tiled=True)
    tiles = ancestors[:, 0, :]
    cell_source = jnp.repeat(tiles, TILE, 1)[:, None, None, :]
    picked = jnp.zeros_like(by_member)
    for member in range(members):
        picked = jnp.where(cell_source == member, by_member[member][None], picked)
    back = lax.all_to_all(picked, "dom", 0, 0, tiled=True)
    return back.reshape(fields, levels, width_x, width_y)


def per_device(ensemble, ancestors, particle_air_drag, eddy_diffusivity):
    _, fields, levels, width_x, width_y = ensemble.shape
    selected = resample(ensemble, ancestors)
    packed = jnp.concatenate(
        [selected.reshape(fields * levels, width_x, width_y), particle_air_drag[0]], axis=0
    )
    lanes = 2 * width_y
    full = with_wide_halo(packed, lanes)
    lane = jnp.arange(lanes, dtype=jnp.int32)
    offset = jnp.where(lane < width_y + 2 * HALO + (lanes - width_y - 2 * HALO) // 2, lane, lane - lanes)
    row_block = lax.axis_index("gy")
    total_rows = width_y * lax.axis_size("gy")
    positions = row_block * width_y + offset
    cor = coriolis_at(positions, total_rows)[None]
    used = (offset < width_y + HALO) & (offset >= -HALO)
    inside = (used & (positions >= 0) & (positions < total_rows)).astype(jnp.float32)[None]
    zero = jnp.zeros((1,), jnp.float32)
    eddy = jnp.concatenate([zero, eddy_diffusivity, zero])
    out = forecast(full, eddy, cor, inside, levels, width_x, width_y)
    return out.reshape(1, fields, levels, width_x, width_y)


def solution(mesh):
    placed = (
        P("dom", None, None, "gx", "gy"),
        P(None, "gx", "gy"),
        P("dom", None, "gx", "gy"),
        P(),
    )
    return jax.shard_map(
        per_device,
        mesh=mesh,
        in_specs=placed,
        out_specs=P("dom", None, None, "gx", "gy"),
        check_vma=False,
    )
```

```python
import jax
import jax.numpy as jnp
from jax import lax
from jax.sharding import PartitionSpec as P
from jax.experimental import pallas as pl
from jax.experimental.pallas import tpu as pltpu


STEPS = 4
TILE = 8


ADVECT = 0.2
DIFFUSE = 0.15
BUOY_TEMP = 0.2
BUOY_SALT = 0.1
PRESS_SCALE = 0.25
WIND_SCALE = 0.2
CORIO_BASE = 0.1
CORIO_SLOPE = 0.1


HALO = STEPS


def shift_pairs(axis, wrap):
    size = lax.axis_size(axis)
    up = [(i, (i + 1) % size) for i in range(size if wrap else size - 1)]
    return up, [(j, i) for i, j in up]


def with_wide_halo(packed, lanes):
    x_up, x_down = shift_pairs("gx", True)
    width_x = packed.shape[1]
    west = lax.ppermute(packed[:, width_x - HALO:, :], "gx", x_up)
    east = lax.ppermute(packed[:, :HALO, :], "gx", x_down)
    rows = jnp.concatenate([packed, east, west], axis=1)
    y_up, y_down = shift_pairs("gy", False)
    width_y = rows.shape[2]
    south = lax.ppermute(rows[:, :, width_y - HALO:], "gy", y_up)
    north = lax.ppermute(rows[:, :, :HALO], "gy", y_down)
    gap = jnp.zeros(rows.shape[:2] + (lanes - width_y - 2 * HALO,), rows.dtype)
    return jnp.concatenate([rows, north, gap, south], axis=2)


def forecast_kernel(levels, eddy_ref, cor_ref, mask_ref, full_ref, out_ref, buf0, buf1):
    n_rows, lanes = full_ref.shape[1], full_ref.shape[2]
    wx, wy = out_ref.shape[1], out_ref.shape[2]

    cor = cor_ref[...]
    inside = mask_ref[...] > 0.5
    state_rows = 4 * levels
    drag = [WIND_SCALE * full_ref[state_rows + i] for i in range(2)]

    def around(a):
        return (
            pltpu.roll(a, n_rows - 1, 0),
            pltpu.roll(a, 1, 0),
            pltpu.roll(a, lanes - 1, 1),
            pltpu.roll(a, 1, 1),
        )

    row8 = lax.broadcasted_iota(jnp.int32, (wx, wy), 0)
    lane8 = lax.broadcasted_iota(jnp.int32, (wx, wy), 1)

    def around_block(lo, nx, hi):
        return (
            jnp.where(row8 == wx - 1, pltpu.roll(nx, wx - 1, 0), pltpu.roll(lo, wx - 1, 0)),
            jnp.where(row8 == 0, pltpu.roll(nx, 1, 0), pltpu.roll(lo, 1, 0)),
            jnp.where(lane8 == wy - 1, pltpu.roll(hi, wy - 1, 1), pltpu.roll(lo, wy - 1, 1)),
            jnp.where(lane8 == 0, pltpu.roll(hi, 1, 1), pltpu.roll(lo, 1, 1)),
        )

    def tendencies(k, c, up, dn, nb, total, nbt, cor_k, drag_k):
        e_up = eddy_ref[k + 1]
        e_dn = eddy_ref[k]
        east_vel, north_vel = c[0], c[1]
        new = []
        for f in range(4):
            e, w, n, s = nb[f]
            spread = e + w + n + s - 4.0 * c[f]
            vertical = e_up * (up[f] - c[f]) - e_dn * (c[f] - dn[f])
            carried = east_vel * (e - w) + north_vel * (n - s)
            new.append(c[f] - (0.5 * ADVECT) * carried + DIFFUSE * spread + vertical)
        pe, pw, pn, ps = nbt
        top = jnp.where(k == 0, 1.0, 0.0).astype(jnp.float32)
        new[0] = new[0] + cor_k * north_vel - (0.5 * PRESS_SCALE) * (pe - pw) + drag_k[0] * top
        new[1] = new[1] - cor_k * east_vel - (0.5 * PRESS_SCALE) * (pn - ps) + drag_k[1] * top
        return new

    def one_step(src, dst):
        def level(k, total):
            above = jnp.minimum(k + 1, levels - 1)
            below = jnp.maximum(k - 1, 0)
            c = [src[f * levels + k] for f in range(4)]
            up = [src[f * levels + above] for f in range(4)]
            dn = [src[f * levels + below] for f in range(4)]
            total = total + (BUOY_TEMP * c[2] - BUOY_SALT * c[3])
            nb = [around(c[f]) for f in range(4)]
            new = tendencies(k, c, up, dn, nb, total, around(total), cor, drag)
            for f in range(4):
                dst[f * levels + k] = jnp.where(inside, new[f], 0.0)
            return total

        lax.fori_loop(0, levels, level, jnp.zeros((n_rows, lanes), jnp.float32), unroll=True)

    def last_step(src):
        def pieces(i):
            return (src[i, :wx, :wy], src[i, wx:, :wy], src[i, :wx, wy:])

        drag_b = [d[:wx, :wy] for d in drag]
        cor_b = cor[:, :wy]

        def level(k, totals):
            above = jnp.minimum(k + 1, levels - 1)
            below = jnp.maximum(k - 1, 0)
            cp = [pieces(f * levels + k) for f in range(4)]
            c = [p[0] for p in cp]
            up = [src[f * levels + above, :wx, :wy] for f in range(4)]
            dn = [src[f * levels + below, :wx, :wy] for f in range(4)]
            totals = tuple(
                t + (BUOY_TEMP * a - BUOY_SALT * b) for t, a, b in zip(totals, cp[2], cp[3])
            )
            nb = [around_block(*p) for p in cp]
            new = tendencies(k, c, up, dn, nb, totals[0], around_block(*totals), cor_b, drag_b)
            for f in range(4):
                out_ref[f * levels + k] = new[f]
            return totals

        zero = jnp.zeros((wx, wy), jnp.float32)
        lax.fori_loop(0, levels, level, (zero, zero, zero), unroll=True)

    one_step(full_ref, buf1)
    one_step(buf1, buf0)
    one_step(buf0, buf1)
    last_step(buf1)


def forecast(full, eddy, cor, inside, levels, width_x, width_y):
    state_rows, rows, lanes = 4 * levels, full.shape[1], full.shape[2]
    kernel = lambda *refs: forecast_kernel(levels, *refs)
    vmem = pl.BlockSpec(memory_space=pltpu.VMEM)
    cells = state_rows * rows * lanes
    return pl.pallas_call(
        kernel,
        out_shape=jax.ShapeDtypeStruct((state_rows, width_x, width_y), jnp.float32),
        in_specs=[pl.BlockSpec(memory_space=pltpu.SMEM), vmem, vmem, vmem],
        out_specs=vmem,
        scratch_shapes=[pltpu.VMEM((state_rows, rows, lanes), jnp.float32)] * 2,
        compiler_params=pltpu.CompilerParams(allow_input_fusion=[False, False, False, True]),
        cost_estimate=pl.CostEstimate(
            flops=STEPS * cells * 40, transcendentals=0,
            bytes_accessed=full.size * 4 + state_rows * width_x * width_y * 4,
        ),
    )(eddy, cor, inside, full)


def coriolis_at(positions, total_rows):
    return CORIO_BASE + CORIO_SLOPE * (positions.astype(jnp.float32) + 0.5) / total_rows


def resample(ensemble, ancestors):
    members = lax.axis_size("dom")
    block = ensemble[0]
    fields, levels, width_x, width_y = block.shape
    groups = fields * levels // members
    parts = block.reshape(members, groups, width_x, width_y)
    by_member = lax.all_to_all(parts, "dom", 0, 0, tiled=True)
    tiles = ancestors[:, 0, :]
    cell_source = jnp.repeat(tiles, TILE, 1)[:, None, None, :]
    picked = jnp.zeros_like(by_member)
    for member in range(members):
        picked = jnp.where(cell_source == member, by_member[member][None], picked)
    back = lax.all_to_all(picked, "dom", 0, 0, tiled=True)
    return back.reshape(fields, levels, width_x, width_y)


def per_device(ensemble, ancestors, particle_air_drag, eddy_diffusivity):
    _, fields, levels, width_x, width_y = ensemble.shape
    selected = resample(ensemble, ancestors)
    packed = jnp.concatenate(
        [selected.reshape(fields * levels, width_x, width_y), particle_air_drag[0]], axis=0
    )
    lanes = 2 * width_y
    full = with_wide_halo(packed, lanes)
    lane = jnp.arange(lanes, dtype=jnp.int32)
    offset = jnp.where(lane < width_y + 2 * HALO + (lanes - width_y - 2 * HALO) // 2, lane, lane - lanes)
    row_block = lax.axis_index("gy")
    total_rows = width_y * lax.axis_size("gy")
    positions = row_block * width_y + offset
    cor = coriolis_at(positions, total_rows)[None]
    used = (offset < width_y + HALO) & (offset >= -HALO)
    inside = (used & (positions >= 0) & (positions < total_rows)).astype(jnp.float32)[None]
    zero = jnp.zeros((1,), jnp.float32)
    eddy = jnp.concatenate([zero, eddy_diffusivity, zero])
    out = forecast(full, eddy, cor, inside, levels, width_x, width_y)
    return out.reshape(1, fields, levels, width_x, width_y)


def solution(mesh):
    placed = (
        P("dom", None, None, "gx", "gy"),
        P(None, "gx", "gy"),
        P("dom", None, "gx", "gy"),
        P(),
    )
    return jax.shard_map(
        per_device,
        mesh=mesh,
        in_specs=placed,
        out_specs=P("dom", None, None, "gx", "gy"),
        check_vma=False,
    )
```
